32 devices in a mesh: kz: 8 (over z, x), en: 4 (over y, core).
Axes of the slice: x: 2, y: 2, z: 4, core: 2. Of those that a mesh axis runs over, the one named last changes fastest.
Arguments:
- green_real: bfloat16 [8, 96, 128, 128], P('kz', 'en'), may hold values from -6 to 6
- green_imag: bfloat16 [8, 96, 128, 128], P('kz', 'en'), may hold values from -6 to 6
- coupling: bfloat16 [2, 4, 8, 128, 128], P(None, None, 'kz'), may hold values from -0.5 to 0.5
- strengths: float32 [2, 4, 8], replicated, may hold values from 0.1 to 1
- offsets: int32 [2, 8], replicated, may hold values from -4 to 4, as said below
Outputs:
- dressed_real: bfloat16 [8, 96, 128, 128], P('kz', 'en')
- dressed_imag: bfloat16 [8, 96, 128, 128], P('kz', 'en')
The draws below stay inside these ranges and needn't reach their ends.
Inputs may be any that keep to these rules, and one draw needn't show every extreme that they name: Each row of offsets holds each of -4 to -1 and 1 to 4 exactly once.
All inputs are finite; a program needn't handle non-finite values.
Results may differ from the reference program's by a relative error of at most 0.007.
Values may be sent and summed in bfloat16 or wider, within the bound.
A program may use at most 128 MiB of HBM per device.

```python
import math
import jax
import jax.numpy as jnp
from jax import lax

NO = 128
REACH = 4
HOPS = 2
BRANCHES = 4
OFFS = 8
NK = 8
NE = 96


def draw_offsets(key, part):
    base_list = jnp.concatenate([jnp.arange(-REACH, 0), jnp.arange(1, REACH + 1)]).astype(jnp.int32)
    key_list = jax.random.split(key, HOPS)
    rows_list = [jax.random.permutation(key_list[hop_index], base_list) for hop_index in range(HOPS)]
    return jnp.stack(rows_list).astype(jnp.int32)


def steps_of(key, dims, shards, least, largest):
    gain, own = 1.0, jax.random.fold_in(key, 6)
    for dim, parts in shards:
        draws = jnp.exp(jax.random.uniform(jax.random.fold_in(own, dim), (parts,), jnp.float32, least / len(shards), largest / len(shards)))
        gain = gain * jnp.repeat(draws, dims[dim] // parts).reshape([-1 if axis == dim else 1 for axis in range(len(dims))])
    return gain


def noise(own_key, extent, spread, bound, pieces=(), dtype=jnp.bfloat16):
    factor_of = steps_of(own_key, extent, pieces, -0.22, 0.18) if pieces else 1.0
    result = jax.random.normal(own_key, extent, jnp.float32) * spread * factor_of
    return jnp.minimum(jnp.maximum(result, -bound), bound).astype(dtype)


def setup_inputs(seed: int = 0) -> dict:
    splits = jax.random.split(jax.random.key(seed), 6)
    green_real = noise(splits[0], (NK, NE, NO, NO), 1.0, 6.0, ((0, 8), (1, 4)))
    green_imag = noise(splits[1], (NK, NE, NO, NO), 1.0, 6.0, ((0, 8), (1, 4)))
    coupling = noise(splits[2], (HOPS, BRANCHES, NK, NO, NO), NO ** -0.5, 0.5, ((2, 8),))
    strengths = jnp.clip(jnp.exp(jax.random.uniform(splits[3], (HOPS, BRANCHES, OFFS), jnp.float32, math.log(0.1), math.log(1.0))), 0.1, 1.0)
    offsets = draw_offsets(jax.random.fold_in(splits[5], 71), 0)
    return dict(green_real=green_real, green_imag=green_imag, coupling=coupling, strengths=strengths, offsets=offsets)


def reference(green_real, green_imag, coupling, strengths, offsets):
    stacked = jnp.stack([green_real, green_imag], axis=1)
    levels = jnp.arange(-REACH, REACH + 1).astype(jnp.int32)
    match_table = (offsets[:, None, :, None] == levels[None, None, None, :]).astype(jnp.float32)
    weights_table = jnp.sum(strengths[:, :, :, None] * match_table, axis=2)

    def per_momentum(momentum):
        own_block = lax.dynamic_index_in_dim(stacked, momentum, 0, keepdims=False).astype(jnp.float32)
        self_energy = jnp.zeros(own_block.shape, jnp.float32)
        for hop_index in range(HOPS):
            source = lax.dynamic_index_in_dim(stacked, ((momentum - hop_index - 1) % NK).astype(jnp.int32), 0, keepdims=False).astype(jnp.float32)
            padded = jnp.pad(source, ((0, 0), (REACH, REACH), (0, 0), (0, 0)))
            for branch_index in range(BRANCHES):
                summed_block = jnp.zeros(own_block.shape, jnp.float32)
                for step_index in range(2 * REACH + 1):
                    energy_shift = step_index - REACH
                    if energy_shift == 0:
                        continue
                    summed_block = summed_block + weights_table[hop_index, branch_index, step_index] * padded[:, REACH - energy_shift:REACH - energy_shift + NE]
                summed_block = lax.optimization_barrier(summed_block.astype(jnp.bfloat16)).astype(jnp.float32)
                matrix = lax.dynamic_index_in_dim(coupling[hop_index, branch_index], momentum, 0, keepdims=False).astype(jnp.float32)
                left_prod = jnp.einsum("ab,xebc->xeac", matrix, summed_block)
                left_prod = lax.optimization_barrier(left_prod.astype(jnp.bfloat16)).astype(jnp.float32)
                self_energy = self_energy + jnp.einsum("xeab,cb->xeac", left_prod, matrix)
        self_energy = lax.optimization_barrier(self_energy.astype(jnp.bfloat16)).astype(jnp.float32)
        real_part = own_block[0]
        imag_part = own_block[1]
        self_real = self_energy[0]
        self_imag = self_energy[1]
        prod_real = jnp.einsum("eab,ebc->eac", real_part, self_real) - jnp.einsum("eab,ebc->eac", imag_part, self_imag)
        prod_imag = jnp.einsum("eab,ebc->eac", real_part, self_imag) + jnp.einsum("eab,ebc->eac", imag_part, self_real)
        prod_real = lax.optimization_barrier(prod_real.astype(jnp.bfloat16)).astype(jnp.float32)
        prod_imag = lax.optimization_barrier(prod_imag.astype(jnp.bfloat16)).astype(jnp.float32)
        back_real = jnp.einsum("eab,ebc->eac", prod_real, real_part) - jnp.einsum("eab,ebc->eac", prod_imag, imag_part)
        back_imag = jnp.einsum("eab,ebc->eac", prod_real, imag_part) + jnp.einsum("eab,ebc->eac", prod_imag, real_part)
        dressed_real = (real_part + back_real / NO).astype(jnp.bfloat16)
        dressed_imag = (imag_part + back_imag / NO).astype(jnp.bfloat16)
        return jnp.stack([dressed_real, dressed_imag])

    results = lax.map(per_momentum, jnp.arange(NK).astype(jnp.int32))
    return (results[:, 0], results[:, 1])
```

```python
import functools

import jax
import jax.numpy as jnp
from jax import lax
from jax.experimental import pallas as pl
from jax.experimental.pallas import tpu as pltpu
from jax.sharding import PartitionSpec as P

REACH = 4
TILE = 32
GROUP = 2
MESH = pl.DeviceIdType.MESH


def kernel(counts, real_hbm, imag_hbm, coupling, strengths, offsets, out_real, out_imag,
           own, near, far, turned, weights, summed,
           own_sem, far_send, far_recv, near_send, near_recv, halo_send, halo_recv):
    momenta, sections = counts
    hops, branches, orbitals = coupling.shape[0], coupling.shape[1], coupling.shape[-1]
    energies = own.shape[1]
    chunks = energies // REACH
    kz, en = lax.axis_index("kz"), lax.axis_index("en")
    odd = lax.rem(kz, 2)
    partner = kz + 1 - 2 * odd
    ahead, behind = lax.rem(kz + 2, momenta), lax.rem(kz + momenta - 2, momenta)
    has_low, has_high = en > 0, en < sections - 1
    sources = (real_hbm, imag_hbm)
    fields = (near, far)

    barrier = pltpu.get_barrier_semaphore()
    for other in (partner, ahead, behind):
        pl.semaphore_signal(barrier, inc=1, device_id=(other, en), device_id_type=MESH)

    @pl.when(has_low)
    def _():
        pl.semaphore_signal(barrier, inc=1, device_id=(kz, en - 1), device_id_type=MESH)

    @pl.when(has_high)
    def _():
        pl.semaphore_signal(barrier, inc=1, device_id=(kz, en + 1), device_id_type=MESH)

    pl.semaphore_wait(barrier, 3 + has_low.astype(jnp.int32) + has_high.astype(jnp.int32))

    def rows(chunk):
        return pl.ds(REACH + chunk * REACH, REACH)

    def far_copy(chunk, part):
        return pltpu.make_async_remote_copy(
            sources[part].at[0, pl.ds(chunk * REACH, REACH)], far.at[part, rows(chunk)],
            far_send.at[chunk, part], far_recv.at[chunk, part],
            device_id=(ahead, en), device_id_type=MESH)

    def near_copy(chunk, part, relay):
        source = far.at[part, rows(chunk)] if relay else sources[part].at[0, pl.ds(chunk * REACH, REACH)]
        return pltpu.make_async_remote_copy(
            source, near.at[part, rows(chunk)],
            near_send.at[chunk, part], near_recv.at[chunk, part],
            device_id=(partner, en), device_id_type=MESH)

    def halo_copy(hop, side, part):
        field = fields[hop]
        if side == 0:
            source, target, to = energies, 0, lax.rem(en + 1, sections)
        else:
            source, target, to = REACH, REACH + energies, lax.rem(en + sections - 1, sections)
        return pltpu.make_async_remote_copy(
            field.at[part, pl.ds(source, REACH)], field.at[part, pl.ds(target, REACH)],
            halo_send.at[hop, side, part], halo_recv.at[hop, side, part],
            device_id=(kz, to), device_id_type=MESH)

    order = [chunks - 1] + list(range(chunks - 1))
    for chunk in order:
        for part in range(2):
            far_copy(chunk, part).start()

    @pl.when(odd == 0)
    def _():
        for chunk in order:
            for part in range(2):
                near_copy(chunk, part, False).start()

    locals_ = [pltpu.make_async_copy(sources[part].at[0], own.at[part], own_sem.at[part]) for part in range(2)]
    for copy in locals_:
        copy.start()

    zeros = jnp.zeros((2, REACH, orbitals, orbitals), jnp.bfloat16)

    @pl.when(en == 0)
    def _():
        near[:, pl.ds(0, REACH)] = zeros
        far[:, pl.ds(0, REACH)] = zeros

    @pl.when(en == sections - 1)
    def _():
        near[:, pl.ds(REACH + energies, REACH)] = zeros
        far[:, pl.ds(REACH + energies, REACH)] = zeros

    for hop in range(hops):
        for branch in range(branches):
            turned[hop, pl.ds(branch * orbitals, orbitals), :] = (
                coupling[hop, branch, 0].astype(jnp.float32).T.astype(jnp.bfloat16))
            for tap in range(2 * REACH + 1):
                if tap == REACH:
                    continue
                total = jnp.float32(0)
                for place in range(offsets.shape[1]):
                    total = total + jnp.where(
                        offsets[hop, place] == REACH - tap, strengths[hop, branch, place], 0.0)
                weights[hop * branches + branch, tap] = total
    for copy in locals_:
        copy.wait()

    def self_energy(energy, slot):
        total = None
        for hop in range(hops):
            field = fields[hop]
            scale = [[weights[hop * branches + branch, tap] for tap in range(2 * REACH + 1)]
                     for branch in range(branches)]
            for part in range(2):
                for row in range(0, orbitals, TILE):
                    sums = [None] * branches
                    for tap in range(2 * REACH + 1):
                        if tap == REACH:
                            continue
                        window = field[part, energy + tap, row:row + TILE, :].astype(jnp.float32)
                        for branch in range(branches):
                            term = scale[branch][tap] * window
                            sums[branch] = term if sums[branch] is None else sums[branch] + term
                    for branch in range(branches):
                        summed[slot, hop, branch, row:row + TILE, part * orbitals:(part + 1) * orbitals] = (
                            sums[branch].astype(jnp.bfloat16))
            lefts = [
                jnp.dot(coupling[hop, branch, 0], summed[slot, hop, branch],
                        preferred_element_type=jnp.float32).astype(jnp.bfloat16)
                for branch in range(branches)]
            stacked = jnp.concatenate(
                [jnp.concatenate([left[:, :orbitals] for left in lefts], axis=1),
                 jnp.concatenate([left[:, orbitals:] for left in lefts], axis=1)], axis=0)
            term = jnp.dot(stacked, turned[hop], preferred_element_type=jnp.float32)
            total = term if total is None else total + term
        return total.astype(jnp.bfloat16)

    def paired(real, imag):
        return jnp.concatenate(
            [jnp.concatenate([real, imag], axis=1), jnp.concatenate([-imag, real], axis=1)], axis=0)

    def finish(energy, sigma):
        real, imag = own[0, energy], own[1, energy]
        prod = jnp.dot(jnp.concatenate([real, imag], axis=1),
                       paired(sigma[:orbitals], sigma[orbitals:]),
                       preferred_element_type=jnp.float32).astype(jnp.bfloat16)
        back = jnp.dot(prod, paired(real, imag), preferred_element_type=jnp.float32) / orbitals
        out_real[0, energy] = (real.astype(jnp.float32) + back[:, :orbitals]).astype(jnp.bfloat16)
        out_imag[0, energy] = (imag.astype(jnp.float32) + back[:, orbitals:]).astype(jnp.bfloat16)

    def compute(first, count):
        def body(index, carry):
            base = first + index * GROUP
            sigmas = [self_energy(base + slot, slot) for slot in range(GROUP)]
            for slot in range(GROUP):
                finish(base + slot, sigmas[slot])
            return carry

        lax.fori_loop(0, count // GROUP, body, 0)

    def halo_out(hop, chunk):
        for side, edge, cond in ((0, chunks - 1, has_high), (1, 0, has_low)):
            if chunk == edge:
                @pl.when(cond)
                def _(side=side):
                    for part in range(2):
                        halo_copy(hop, side, part).start()

    def halo_in(side, cond):
        @pl.when(cond)
        def _():
            for hop in range(hops):
                for part in range(2):
                    halo_copy(hop, side, part).wait_recv()

    for step, chunk in enumerate(order):
        for part in range(2):
            far_copy(chunk, part).wait_recv()

            @pl.when(odd == 1)
            def _(part=part):
                near_copy(chunk, part, True).start()
        halo_out(1, chunk)
        for part in range(2):
            near_copy(chunk, part, False).wait_recv()
        halo_out(0, chunk)
        if step == 2:
            halo_in(0, has_low)
        if step >= 2 and step < chunks - 1:
            compute((chunk - 1) * REACH, REACH)
    halo_in(1, has_high)
    compute((chunks - 3) * REACH, 3 * REACH)

    for chunk in order:
        for part in range(2):
            far_copy(chunk, part).wait_send()
            near_copy(chunk, part, False).wait_send()
    for side, cond in ((0, has_high), (1, has_low)):
        @pl.when(cond)
        def _(side=side):
            for hop in range(hops):
                for part in range(2):
                    halo_copy(hop, side, part).wait_send()


def shards(counts, green_real, green_imag, coupling, strengths, offsets):
    energies, orbitals = green_real.shape[1], green_real.shape[2]
    hops, branches = coupling.shape[0], coupling.shape[1]
    chunks = energies // REACH
    anywhere = pl.BlockSpec(memory_space=pl.ANY)
    vmem = pl.BlockSpec(memory_space=pltpu.VMEM)
    smem = pl.BlockSpec(memory_space=pltpu.SMEM)
    dma = pltpu.SemaphoreType.DMA
    extended = (2, energies + 2 * REACH, orbitals, orbitals)
    return pl.pallas_call(
        functools.partial(kernel, counts),
        out_shape=[jax.ShapeDtypeStruct(green_real.shape, jnp.bfloat16)] * 2,
        in_specs=[anywhere, anywhere, vmem, smem, smem],
        out_specs=[vmem, vmem],
        scratch_shapes=[
            pltpu.VMEM((2, energies, orbitals, orbitals), jnp.bfloat16),
            pltpu.VMEM(extended, jnp.bfloat16),
            pltpu.VMEM(extended, jnp.bfloat16),
            pltpu.VMEM((hops, branches * orbitals, orbitals), jnp.bfloat16),
            pltpu.SMEM((hops * branches, 2 * REACH + 1), jnp.float32),
            pltpu.VMEM((GROUP, hops, branches, orbitals, 2 * orbitals), jnp.bfloat16),
            dma((2,)),
            dma((chunks, 2)), dma((chunks, 2)),
            dma((chunks, 2)), dma((chunks, 2)),
            dma((hops, 2, 2)), dma((hops, 2, 2)),
        ],
        compiler_params=pltpu.CompilerParams(collective_id=0, has_side_effects=True),
    )(green_real, green_imag, coupling, strengths, offsets)


def solution(mesh):
    blocks = P("kz", "en", None, None)
    counts = (mesh.shape["kz"], mesh.shape["en"])
    return jax.shard_map(
        functools.partial(shards, counts), mesh=mesh,
        in_specs=(blocks, blocks, P(None, None, "kz", None, None), P(), P()),
        out_specs=(blocks, blocks), check_vma=False)
```

```python
import functools

import jax
import jax.numpy as jnp
from jax import lax
from jax.experimental import pallas as pl
from jax.experimental.pallas import tpu as pltpu
from jax.sharding import PartitionSpec as P

REACH = 4
TILE = 64
SLOTS = 3
KIND = jnp.bfloat16
LANES = 16
MESH = pl.DeviceIdType.MESH


def pieces_of(energies):
    pieces = [(energies - REACH, REACH), (0, REACH)]
    while sum(size for _, size in pieces) < energies:
        start = pieces[-1][0] + pieces[-1][1]
        pieces.append((start, min(SLOTS, energies - REACH - start)))
    return pieces


def kernel(counts, real_hbm, imag_hbm, coupling, strengths, offsets, out_real, out_imag,
           own, near, far, turned, flat, weights, summed, sigma,
           own_sem, far_send, far_recv, near_send, near_recv, halo_send, halo_recv):
    momenta, sections = counts
    hops, branches, orbitals = coupling.shape[0], coupling.shape[1], coupling.shape[-1]
    energies = own.shape[1]
    pieces = pieces_of(energies)
    kz, en = lax.axis_index("kz"), lax.axis_index("en")
    odd = lax.rem(kz, 2)
    partner = kz + 1 - 2 * odd
    ahead, behind = lax.rem(kz + 2, momenta), lax.rem(kz + momenta - 2, momenta)
    has_low, has_high = en > 0, en < sections - 1
    sources = (real_hbm, imag_hbm)
    fields = (near, far)

    barrier = pltpu.get_barrier_semaphore()
    for other in (partner, ahead, behind):
        pl.semaphore_signal(barrier, inc=1, device_id=(other, en), device_id_type=MESH)

    @pl.when(has_low)
    def _():
        pl.semaphore_signal(barrier, inc=1, device_id=(kz, en - 1), device_id_type=MESH)

    @pl.when(has_high)
    def _():
        pl.semaphore_signal(barrier, inc=1, device_id=(kz, en + 1), device_id_type=MESH)

    pl.semaphore_wait(barrier, 3 + has_low.astype(jnp.int32) + has_high.astype(jnp.int32))

    def rows(piece):
        return pl.ds(REACH + pieces[piece][0], pieces[piece][1])

    def inner(piece, part):
        return sources[part].at[0, pl.ds(*pieces[piece])]

    def far_copy(chunk, part):
        return pltpu.make_async_remote_copy(
            inner(chunk, part), far.at[part, rows(chunk)],
            far_send.at[chunk, part], far_recv.at[chunk, part],
            device_id=(ahead, en), device_id_type=MESH)

    def near_copy(chunk, part, relay):
        source = far.at[part, rows(chunk)] if relay else inner(chunk, part)
        return pltpu.make_async_remote_copy(
            source, near.at[part, rows(chunk)],
            near_send.at[chunk, part], near_recv.at[chunk, part],
            device_id=(partner, en), device_id_type=MESH)

    def halo_copy(hop, side, part):
        field = fields[hop]
        if side == 0:
            source, target, to = energies, 0, lax.rem(en + 1, sections)
        else:
            source, target, to = REACH, REACH + energies, lax.rem(en + sections - 1, sections)
        return pltpu.make_async_remote_copy(
            field.at[part, pl.ds(source, REACH)], field.at[part, pl.ds(target, REACH)],
            halo_send.at[hop, side, part], halo_recv.at[hop, side, part],
            device_id=(kz, to), device_id_type=MESH)

    order = range(len(pieces))
    for chunk in order:
        for part in range(2):
            far_copy(chunk, part).start()

    @pl.when(odd == 0)
    def _():
        for chunk in order:
            for part in range(2):
                near_copy(chunk, part, False).start()

    locals_ = [pltpu.make_async_copy(sources[part].at[0], own.at[part], own_sem.at[part]) for part in range(2)]
    for copy in locals_:
        copy.start()

    zeros = jnp.zeros((2, REACH, orbitals, orbitals), jnp.bfloat16)

    @pl.when(en == 0)
    def _():
        near[:, pl.ds(0, REACH)] = zeros
        far[:, pl.ds(0, REACH)] = zeros

    @pl.when(en == sections - 1)
    def _():
        near[:, pl.ds(REACH + energies, REACH)] = zeros
        far[:, pl.ds(REACH + energies, REACH)] = zeros

    for hop in range(hops):
        for branch in range(branches):
            matrix = coupling[hop, branch, 0]
            side, other = branch % 2 * orbitals, (1 - branch % 2) * orbitals
            turned[hop, branch // 2, side:side + orbitals, side:side + orbitals] = (
                matrix.astype(jnp.float32).T.astype(jnp.bfloat16))
            turned[hop, branch // 2, side:side + orbitals, other:other + orbitals] = jnp.zeros_like(matrix)
            place = (hop * branches + branch) * orbitals
            flat[:, place:place + orbitals] = matrix
            for tap in range(2 * REACH + 1):
                if tap == REACH:
                    continue
                total = jnp.float32(0)
                for index in range(offsets.shape[1]):
                    total = total + jnp.where(
                        offsets[hop, index] == REACH - tap, strengths[hop, branch, index], 0.0)
                weights[(hop * branches + branch) * (2 * REACH + 1) + tap] = jnp.full(
                    (LANES, orbitals), total, jnp.float32).astype(KIND)
    for copy in locals_:
        copy.wait()

    def mix(energy, slot, hop, part, row):
        field = fields[hop]
        sums = [None] * branches
        for tap in range(2 * REACH + 1):
            if tap == REACH:
                continue
            window = field[part, energy + tap, row:row + TILE, :].astype(KIND)
            for branch in range(branches):
                scale = weights[(hop * branches + branch) * (2 * REACH + 1) + tap]
                term = jnp.concatenate([scale] * (TILE // LANES), axis=0) * window
                sums[branch] = term if sums[branch] is None else sums[branch] + term
        for branch in range(branches):
            side = branch % 2 * orbitals
            summed[slot, hop, branch // 2, part * orbitals + row:part * orbitals + row + TILE, side:side + orbitals] = (
                sums[branch].astype(jnp.bfloat16))

    def right(slot, hop, pair):
        both = jnp.dot(summed[slot, hop, pair], turned[hop, pair],
                       preferred_element_type=jnp.float32).astype(jnp.bfloat16)
        return [jnp.concatenate([both[:orbitals, side:side + orbitals], both[orbitals:, side:side + orbitals]], axis=1)
                for side in (0, orbitals)]

    def paired(real, imag):
        return jnp.concatenate(
            [jnp.concatenate([real, imag], axis=1), jnp.concatenate([-imag, real], axis=1)], axis=0)

    def product(energy, slot):
        real, imag = own[0, energy], own[1, energy]
        return jnp.dot(jnp.concatenate([real, imag], axis=1),
                       paired(sigma[slot, :, :orbitals], sigma[slot, :, orbitals:]),
                       preferred_element_type=jnp.float32).astype(jnp.bfloat16)

    def dress(energy, prod):
        real, imag = own[0, energy], own[1, energy]
        back = jnp.dot(prod, paired(real, imag), preferred_element_type=jnp.float32) / orbitals
        out_real[0, energy] = (real.astype(jnp.float32) + back[:, :orbitals]).astype(jnp.bfloat16)
        out_imag[0, energy] = (imag.astype(jnp.float32) + back[:, orbitals:]).astype(jnp.bfloat16)

    def stage(energy, place, mixes=True, lefts=True):
        mix_slot, left_slot, last_slot = place % SLOTS, (place - 1) % SLOTS, (place - 2) % SLOTS
        last = jnp.maximum(energy - 2, 0)
        prod = product(last, last_slot)
        parts = []
        units = [(part, row) for part in range(2) for row in range(0, orbitals, TILE)]
        share = -(-2 * len(units) // branches)
        for hop in range(hops):
            for pair in range(branches // 2):
                if lefts:
                    parts += right(left_slot, hop, pair)
                if mixes:
                    for part, row in units[pair * share:(pair + 1) * share]:
                        mix(energy, mix_slot, hop, part, row)
            if hop == 0:
                dress(last, prod)
        if lefts:
            sigma[left_slot] = jnp.dot(
                flat[...], jnp.concatenate(parts, axis=0), preferred_element_type=jnp.float32).astype(jnp.bfloat16)

    def compute(first, count):
        def body(index, carry):
            for place in range(SLOTS):
                stage(first + index * SLOTS + place, place)
            return carry

        if count == SLOTS:
            body(0, 0)
        else:
            lax.fori_loop(0, count // SLOTS, body, 0)

    def drain():
        stage(energies, 0, mixes=False)
        stage(energies + 1, 1, mixes=False, lefts=False)

    def halo_out(hop, chunk):
        for side, edge, cond in ((0, 0, has_high), (1, 1, has_low)):
            if chunk == edge:
                @pl.when(cond)
                def _(side=side):
                    for part in range(2):
                        halo_copy(hop, side, part).start()

    def halo_in(side, cond):
        @pl.when(cond)
        def _():
            for hop in range(hops):
                for part in range(2):
                    halo_copy(hop, side, part).wait_recv()

    for chunk in order:
        for part in range(2):
            far_copy(chunk, part).wait_recv()

            @pl.when(odd == 1)
            def _(part=part):
                near_copy(chunk, part, True).start()
        halo_out(1, chunk)
        for part in range(2):
            near_copy(chunk, part, False).wait_recv()
        halo_out(0, chunk)
        if chunk == 2:
            halo_in(0, has_low)
        if chunk >= 2 and pieces[chunk][1] == SLOTS:
            compute((chunk - 2) * SLOTS, SLOTS)
    halo_in(1, has_high)
    done = (energies - 2 * REACH) // SLOTS * SLOTS
    compute(done, energies - done)
    drain()

    for chunk in order:
        for part in range(2):
            far_copy(chunk, part).wait_send()
            near_copy(chunk, part, False).wait_send()
    for side, cond in ((0, has_high), (1, has_low)):
        @pl.when(cond)
        def _(side=side):
            for hop in range(hops):
                for part in range(2):
                    halo_copy(hop, side, part).wait_send()


def shards(counts, green_real, green_imag, coupling, strengths, offsets):
    energies, orbitals = green_real.shape[1], green_real.shape[2]
    hops, branches = coupling.shape[0], coupling.shape[1]
    pieces = pieces_of(energies)
    anywhere = pl.BlockSpec(memory_space=pl.ANY)
    vmem = pl.BlockSpec(memory_space=pltpu.VMEM)
    smem = pl.BlockSpec(memory_space=pltpu.SMEM)
    dma = pltpu.SemaphoreType.DMA
    chunks = len(pieces_of(energies))
    extended = (2, energies + 2 * REACH, orbitals, orbitals)
    return pl.pallas_call(
        functools.partial(kernel, counts),
        out_shape=[jax.ShapeDtypeStruct(green_real.shape, jnp.bfloat16)] * 2,
        in_specs=[anywhere, anywhere, vmem, smem, smem],
        out_specs=[vmem, vmem],
        scratch_shapes=[
            pltpu.VMEM((2, energies, orbitals, orbitals), jnp.bfloat16),
            pltpu.VMEM(extended, jnp.bfloat16),
            pltpu.VMEM(extended, jnp.bfloat16),
            pltpu.VMEM((hops, branches // 2, 2 * orbitals, 2 * orbitals), jnp.bfloat16),
            pltpu.VMEM((orbitals, hops * branches * orbitals), jnp.bfloat16),
            pltpu.VMEM((hops * branches * (2 * REACH + 1), LANES, orbitals), KIND),
            pltpu.VMEM((SLOTS, hops, branches // 2, 2 * orbitals, 2 * orbitals), jnp.bfloat16),
            pltpu.VMEM((SLOTS, orbitals, 2 * orbitals), jnp.bfloat16),
            dma((2,)),
            dma((chunks, 2)), dma((chunks, 2)),
            dma((chunks, 2)), dma((chunks, 2)),
            dma((hops, 2, 2)), dma((hops, 2, 2)),
        ],
        compiler_params=pltpu.CompilerParams(
            collective_id=0, has_side_effects=True, vmem_limit_bytes=24 * 2**20),
    )(green_real, green_imag, coupling, strengths, offsets)


def solution(mesh):
    blocks = P("kz", "en", None, None)
    counts = (mesh.shape["kz"], mesh.shape["en"])
    return jax.shard_map(
        functools.partial(shards, counts), mesh=mesh,
        in_specs=(blocks, blocks, P(None, None, "kz", None, None), P(), P()),
        out_specs=(blocks, blocks), check_vma=False)
```
